32 devices in a mesh: dom: 8 (over z, x), attr: 4 (over y, core).
Axes of the slice: x: 2, y: 2, z: 4, core: 2. Of those that a mesh axis runs over, the one named last changes fastest.
Arguments:
- records: bfloat16 [12288, 1024], P('dom', 'attr'), may hold values from -6 to 6
- owner: int32 [12288, 1], P('dom'), may hold values from 0 to 7; in each aligned block of 1536 rows (0 to 1535, 1536 to 3071, ...) at most 384 rows name the same one
- entity_means: bfloat16 [4096, 1024], P('dom', 'attr'), may hold values from -6 to 6
- noise_bits: int32 [24576, 512], P('dom'), may hold values from 0 to 8191
Outputs:
- new_means: float32 [4096, 1024], P('dom', 'attr')
- gram: float32 [1024, 1024], P(('dom', 'attr'))
The draws below stay inside these ranges and needn't reach their ends.
Inputs may be any that keep to these rules, and one draw needn't show every extreme that they name: `owner`: among the records of one index of dom at most 384 name the same partition, and in every draw some partition is named by exactly 384 of them.
All inputs are finite; a program needn't handle non-finite values.
Results may differ from the reference program's by a relative error of at most 0.0013.
Values may be sent and summed in bfloat16 or wider, within the bound.
A program may use at most 64 MiB of HBM per device.

```python
import math
import jax
import jax.numpy as jnp
import numpy as np
from jax import lax

E = 1024
ENT_DEV = 512
R_DEV = 1536
CAP = 384
SLOTS = 3072
RECORDS = 12288
ENTITIES = 4096
N_DOM = 8


def touch_ends(array, rng, smallest, largest):
    place = [jax.random.randint(jax.random.fold_in(rng, axis), (), 0, length) for axis, length in enumerate(array.shape)]
    main_axis = array.shape.index(max(array.shape))
    next_to = place[:main_axis] + [(place[main_axis] + 1) % array.shape[main_axis]] + place[main_axis + 1:]
    return array.at[tuple(place)].set(smallest).at[tuple(next_to)].set(largest)


def strengthened(drawn, own_key, source, target, blocks, factor):
    owner, partner = [(jnp.arange(drawn.shape[dim]) // (drawn.shape[dim] // blocks)).reshape([-1 if axis == dim else 1 for axis in range(drawn.ndim)]) for dim in (source, target)]
    chosen = jax.random.permutation(own_key, blocks)[partner]
    strong = (owner == chosen) | (owner == (partner + blocks // 2) % blocks)
    return jnp.where(strong, factor * drawn, drawn)


def level_of(rng, shape, pieces, low, high):
    loudness, own = 1.0, jax.random.fold_in(rng, 6)
    for dim, shards_of in pieces:
        heights = jnp.exp(jax.random.uniform(jax.random.fold_in(own, dim), (shards_of,), jnp.float32, low / len(pieces), high / len(pieces)))
        loudness = loudness * jnp.repeat(heights, shape[dim] // shards_of).reshape([-1 if axis == dim else 1 for axis in range(len(shape))])
    return loudness


def assign_block(stream_key, own, number, rows, count, top, limit, lean):
    sequence = jax.random.permutation(stream_key, count)
    heavy_load, usual = shares(count, rows * top, limit, lean, True), shares(count, rows * top, limit, lean, False)
    places = jnp.arange(count)

    def named(lengths, turn):
        used = int((lengths > 0).sum())
        fixed = max(1, used // 4)
        moved = fixed + (places - fixed + turn * (used - fixed)) % max(1, count - fixed)
        return jnp.zeros((count,), jnp.int32).at[sequence[jnp.where(places < fixed, places, moved)]].set(jnp.asarray(lengths, jnp.int32))

    lengths = jnp.where(number % 4 == 0, named(heavy_load, number // 4), named(usual, number - number // 4 - 1))
    mixed = jax.random.permutation(jax.random.fold_in(own, 3), count)
    source_of, sink = mixed[0:count // 2 * 2:2], mixed[1:count // 2 * 2:2]
    margin = jnp.minimum(lengths[source_of] - 1, limit - lengths[sink]) // 2
    margin = jnp.where((source_of == sequence[0]) | (sink == sequence[0]) | (lengths[sink] == 0), 0, jnp.maximum(margin, 0))
    moved = jax.random.randint(jax.random.fold_in(own, 4), (count // 2,), 0, 1 << 20) % (margin + 1)
    lengths = lengths.at[source_of].add(-moved).at[sink].add(moved)
    items = jnp.searchsorted(jnp.cumsum(lengths), jnp.arange(rows * top), side="right").astype(jnp.int32)
    table = items.reshape(top, rows).T
    table = table[jax.random.permutation(jax.random.fold_in(own, 1), rows)]
    turn = jax.random.randint(jax.random.fold_in(own, 2), (rows, 1), 0, top)
    return jnp.take_along_axis(table, (jnp.arange(top)[None, :] + turn) % top, axis=1)


def shares(amount, total, limit, skew, full):
    loads = [(1 << 20) // math.isqrt(grade ** skew) + 1 for grade in range(1, amount + 1)]
    largest = limit if full else min(limit, max(-(-total // amount), total * loads[0] // sum(loads)))
    least = 1 if total - largest >= amount - 1 else 0
    counts, rest = [largest] + [least] * (amount - 1), total - largest - least * (amount - 1)
    while rest > 0:
        movable = [i for i in range(1, amount) if counts[i] < largest] or [i for i in range(1, amount) if counts[i] < limit]
        pool, budget = sum([loads[i] for i in movable]), rest
        for i in movable:
            extra = min(limit - counts[i], max(1, budget * loads[i] // pool), rest)
            counts[i] = counts[i] + extra
            rest = rest - extra
    return np.array(counts)


def scatter_about(own_key, extent, deviation, bound, split=(), held_as=jnp.bfloat16):
    array = jax.random.normal(own_key, extent, jnp.float32) * deviation
    if len(split) > 0:
        array = level_of(own_key, extent, split, -0.22, 0.18) * array
    return jnp.clip(array, min=-bound, max=bound).astype(held_as)


def gaussian_with(own_key, dims, spread, reach, cuts, heavy, kind=jnp.bfloat16):
    values = spread * jax.random.normal(own_key, dims, jnp.float32)
    if cuts:
        values = values * level_of(own_key, dims, cuts, -0.22, 0.18)
    return jnp.clip(strengthened(values, jax.random.fold_in(own_key, 3), *heavy), -reach, reach).astype(kind)


def setup_inputs(seed: int = 0) -> dict:
    key_list = jax.random.split(jax.random.key(seed), 5)
    records = gaussian_with(key_list[0], (RECORDS, E), 1.0, 6.0, ((0, 8), (1, 4)), (0, 1, 8, 2.0))
    owner_keys = jax.random.split(jax.random.fold_in(key_list[1], 1), RECORDS // R_DEV)
    owner_turns = jax.random.permutation(jax.random.fold_in(key_list[1], 3), RECORDS // R_DEV)
    owner = jax.vmap(lambda own, number: assign_block(jax.random.fold_in(key_list[1], 2), own, number, R_DEV, N_DOM, 1, CAP, 2))(owner_keys, owner_turns).reshape((RECORDS, 1))
    entity_means = scatter_about(key_list[2], (ENTITIES, E), 1.0, 6.0, ((0, 8), (1, 4)))
    noise_bits = touch_ends(jax.random.randint(key_list[3], (SLOTS * N_DOM, ENT_DEV), 0, 8192), jax.random.fold_in(key_list[3], 1), 0, 8191).astype(jnp.int32)
    return dict(records=records, owner=owner, entity_means=entity_means, noise_bits=noise_bits)


def posterior(raw, bits, live, width):
    uniform = (bits.astype(jnp.float32) + 0.5) / 8192.0
    noise = -jnp.log(-jnp.log(uniform))
    logits = 3.0 * jnp.tanh(raw * (width ** -0.5)) + noise
    expd = jnp.exp(logits)
    return (expd / jnp.sum(expd, axis=1, keepdims=True) * live[:, None]).astype(jnp.bfloat16)


def reference(records, owner, entity_means, noise_bits):
    dest = owner[:, 0].astype(jnp.int32)
    source = (jnp.arange(RECORDS, dtype=jnp.int32) // R_DEV).astype(jnp.int32)
    onehot = (dest[:, None] == jnp.arange(N_DOM, dtype=jnp.int32)[None, :]).astype(jnp.int32)
    onehot = onehot.reshape(N_DOM, R_DEV, N_DOM)
    running = jnp.cumsum(onehot, axis=1)
    rank = (jnp.sum(running * onehot, axis=2) - 1).reshape(RECORDS).astype(jnp.int32)
    slot = (source * CAP + rank).astype(jnp.int32)

    def per_owner(gram_total, part):
        position = jnp.where(dest == part, slot, SLOTS).astype(jnp.int32)
        buffer = jnp.zeros((SLOTS + 1, E), jnp.bfloat16).at[position].set(records)[:SLOTS]
        live = jnp.zeros((SLOTS + 1,), jnp.float32).at[position].set(1.0)[:SLOTS]
        means = lax.dynamic_slice(entity_means, ((part * ENT_DEV).astype(jnp.int32), jnp.int32(0)), (ENT_DEV, E))
        bits = lax.dynamic_slice(noise_bits, ((part * SLOTS).astype(jnp.int32), jnp.int32(0)), (SLOTS, ENT_DEV))
        raw = jnp.dot(buffer, means.T, preferred_element_type=jnp.float32)
        weights = posterior(raw, bits, live, E)
        sums = jnp.dot(weights.T, buffer, preferred_element_type=jnp.float32)
        mass = jnp.sum(weights.astype(jnp.float32), axis=0)
        updated = (sums + 1.0 * means.astype(jnp.float32)) / (mass[:, None] + 1.0)
        recon = jnp.dot(weights, means, preferred_element_type=jnp.float32)
        residual = ((buffer.astype(jnp.float32) - recon) * live[:, None]).astype(jnp.bfloat16)
        term = jnp.dot(residual.T, residual, preferred_element_type=jnp.float32)
        return gram_total + term, updated

    gram_total, updated = lax.scan(per_owner, jnp.zeros((E, E), jnp.float32), jnp.arange(N_DOM, dtype=jnp.int32))
    return updated.reshape(ENTITIES, E), gram_total / RECORDS
```

```python
import functools

import jax
import jax.numpy as jnp
from jax import lax
from jax.experimental import pallas as pl
from jax.experimental.pallas import tpu as pltpu
from jax.sharding import PartitionSpec as P


def posterior(raw, bits, live, width):
    uniform = (bits.astype(jnp.float32) + 0.5) / 8192.0
    noise = -jnp.log(-jnp.log(uniform))
    logits = 3.0 * jnp.tanh(raw * width ** (-0.5)) + noise
    expd = jnp.exp(logits)
    return (expd / jnp.sum(expd, axis=1, keepdims=True) * live[:, None]).astype(jnp.bfloat16)


def shards(records, owner, entity_means, noise_bits):
    dom_count = lax.axis_size("dom")
    attr_count = lax.axis_size("attr")
    rec_dev, feat_cols = records.shape
    slot_count = 2 * rec_dev
    capacity = slot_count // dom_count
    width = feat_cols * attr_count
    total_records = rec_dev * dom_count
    dest = owner[:, 0]
    onehot = (dest[:, None] == jnp.arange(dom_count, dtype=jnp.int32)[None, :]).astype(jnp.int32)
    rank = jnp.sum(jnp.cumsum(onehot, axis=0) * onehot, axis=1) - 1
    position = dest * capacity + rank
    packed = jnp.zeros((slot_count, feat_cols), jnp.bfloat16).at[position].set(records)
    flag_buf = (
        jnp.zeros((slot_count,), jnp.bfloat16).at[position].set(jnp.ones((rec_dev,), jnp.bfloat16))
    )
    arrived, arrived_flags = (
        lax.all_to_all(
            packed.reshape(dom_count, capacity, feat_cols),
            "dom",
            split_axis=0,
            concat_axis=0,
            tiled=True,
        ),
        lax.all_to_all(
            flag_buf.reshape(dom_count, capacity), "dom", split_axis=0, concat_axis=0, tiled=True
        ),
    )
    arrived = arrived.reshape(slot_count, feat_cols)
    live = arrived_flags.reshape(slot_count).astype(jnp.float32)
    raw = lax.psum(jnp.dot(arrived, entity_means.T, preferred_element_type=jnp.float32), "attr")
    weights = posterior(raw, noise_bits, live, width)
    sums_cols = jnp.dot(weights.T, arrived, preferred_element_type=jnp.float32)
    mass_col = jnp.sum(weights.astype(jnp.float32), axis=0)[:, None]
    recon = jnp.dot(weights, entity_means, preferred_element_type=jnp.float32)
    col_resid = ((arrived.astype(jnp.float32) - recon) * live[:, None]).astype(jnp.bfloat16)
    residual = lax.all_to_all(col_resid, "attr", split_axis=0, concat_axis=1, tiled=True)
    new_means = (sums_cols + 1.0 * entity_means.astype(jnp.float32)) / (mass_col + 1.0)
    term = lax.dot_general(
        residual, residual, (((0,), (0,)), ((), ())), preferred_element_type=jnp.float32
    )
    gram = lax.psum_scatter(term / total_records, ("dom", "attr"), scatter_dimension=0, tiled=True)
    return (new_means, gram)

MESH = pl.DeviceIdType.MESH
F32, BF16 = jnp.float32, jnp.bfloat16
GROUP = 2


def nt(a, b):
    return lax.dot_general(a, b, (((1,), (1,)), ((), ())), preferred_element_type=F32)


def nn(a, b):
    return jnp.dot(a, b, preferred_element_type=F32)


def remote(src, dst, send_sem, recv_sem, dev):
    return pltpu.make_async_remote_copy(
        src_ref=src, dst_ref=dst, send_sem=send_sem, recv_sem=recv_sem, device_id=dev, device_id_type=MESH
    )


def sweep_kernel(
    n, na, owner_ref, records_ref, means_ref, noise_ref, new_ref, gram_ref,
    rank_ref, meta_ref, metas, packed, x_ref, m_ref, bits_ref, w_ref, wt_ref, r_ref, rt_ref,
    mass_ref, masses, s_send, s_keep, s_recv, s_send2, s_recv2,
    g_send, g_keep, g_recv, gx_send, gx_recv, gy_send, gy_recv, gz_send, gz_recv,
    rec_send, rec_recv, meta_send, meta_recv, mean_send, mean_recv, bits_sem,
    mass_send, mass_recv, st_send, st_recv, gz_ssem, gz_rsem,
):
    rec_dev, feats = records_ref.shape
    ents = means_ref.shape[0]
    cap = 2 * rec_dev // n
    sub = cap // na
    half = n // 2
    width = feats * na
    d, q = lax.axis_index("dom"), lax.axis_index("attr")
    me = d * na + q
    total = n * na

    barrier = pltpu.get_barrier_semaphore()

    @pl.loop(1, total)
    def _(i):
        dev = lax.rem(me + i, total)
        pl.semaphore_signal(barrier, inc=1, device_id=(dev // na, lax.rem(dev, na)), device_id_type=MESH)

    def bits_copy(k):
        s = lax.rem(d + half + n - k, n)
        rows = pl.ds(pl.multiple_of(s * cap + q * sub, sub), sub)
        return pltpu.make_async_copy(
            noise_ref.at[rows, :], bits_ref.at[pl.ds(pl.multiple_of(k * sub, sub), sub), :], bits_sem.at[k]
        )

    @pl.loop(0, n)
    def _(k):
        bits_copy(k).start()

    blk = 256
    ids = lax.broadcasted_iota(jnp.int32, (n, blk), 0)
    upper = (
        lax.broadcasted_iota(jnp.int32, (blk, blk), 0) <= lax.broadcasted_iota(jnp.int32, (blk, blk), 1)
    ).astype(F32).astype(BF16)
    carry = jnp.zeros((n, 1), F32)
    for b in range(rec_dev // blk):
        cols = slice(b * blk, (b + 1) * blk)
        hot = (ids == owner_ref[:, cols]).astype(F32)
        run = nn(hot.astype(BF16), upper) + carry
        rank_ref[:, cols] = (jnp.sum(run * hot, axis=0, keepdims=True) - 1.0).astype(jnp.int32)
        carry = carry + jnp.sum(hot, axis=1, keepdims=True)
    counts = jnp.broadcast_to(carry, (n, 128)).astype(jnp.int32)
    meta_ref[...] = counts
    metas[half] = counts
    m_ref[q] = means_ref[...]

    pl.semaphore_wait(barrier, total - 1)

    def mean_copy(j, peer):
        return remote(means_ref, m_ref.at[q], mean_send.at[j], mean_recv.at[q], (d, peer))

    for j in range(1, na):
        mean_copy(j, lax.rem(q + j, na)).start()

    def meta_copy(k):
        return remote(meta_ref, metas.at[k], meta_send.at[k], meta_recv.at[k], (lax.rem(d + half + k, n), q))

    def rec_copy(k, j, peer_d):
        return remote(
            packed.at[k, pl.ds(j * sub, sub), :],
            x_ref.at[q, pl.ds(pl.multiple_of(k * sub, sub), sub), :],
            rec_send.at[k, j], rec_recv.at[k, q], (peer_d, j),
        )

    @pl.loop(0, n)
    def _(k):
        o = lax.rem(d + half + k, n)
        pos = jnp.where(owner_ref[...] == o, rank_ref[...], -1)
        hot = (lax.broadcasted_iota(jnp.int32, (cap, rec_dev), 0) == pos).astype(F32).astype(BF16)
        packed[k] = nn(hot, records_ref[...]).astype(BF16)

        @pl.when(k != half)
        def _():
            meta_copy(k).start()

        for j in range(na):
            mine = jnp.logical_and(k == half, q == j)

            @pl.when(jnp.logical_not(mine))
            def _():
                rec_copy(k, j, o).start()

            @pl.when(mine)
            def _():
                x_ref[j, pl.ds(pl.multiple_of(k * sub, sub), sub), :] = packed[k, pl.ds(j * sub, sub), :]

    for j in range(1, na):
        src = lax.rem(q + j, na)
        remote(means_ref, m_ref.at[src], mean_send.at[j], mean_recv.at[src], (d, src)).wait_recv()

    rows = GROUP * sub
    mass_ref[...] = jnp.zeros_like(mass_ref)

    @pl.loop(0, n // GROUP)
    def _(g):
        for t in range(GROUP):
            k = g * GROUP + t

            @pl.when(k != half)
            def _():
                meta_copy(k).wait_recv()

            bits_copy(k).wait()
            for a in range(na):
                @pl.when(jnp.logical_not(jnp.logical_and(k == half, q == a)))
                def _():
                    remote(
                        packed.at[k, pl.ds(0, sub), :],
                        x_ref.at[a, pl.ds(pl.multiple_of(k * sub, sub), sub), :],
                        rec_send.at[k, a], rec_recv.at[k, a], (d, a),
                    ).wait_recv()

        at = pl.ds(pl.multiple_of(g * rows, rows), rows)
        raw = nt(x_ref[0, at, :], m_ref[0])
        for a in range(1, na):
            raw = raw + nt(x_ref[a, at, :], m_ref[a])
        uniform = (bits_ref[at, :].astype(F32) + 0.5) / 8192.0
        expd = jnp.exp(3.0 * jnp.tanh(raw * width ** (-0.5))) / (-jnp.log(uniform))
        row = lax.broadcasted_iota(jnp.int32, (rows, 1), 0)
        live = jnp.zeros((rows, 1), F32)
        for t in range(GROUP):
            cnt = metas[g * GROUP + t, pl.ds(d, 1), :][:, :1]
            inside = jnp.logical_and(row >= t * sub, row < (t + 1) * sub)
            live = live + jnp.where(jnp.logical_and(inside, row - t * sub + q * sub < cnt), 1.0, 0.0)
        w = (expd * (live / jnp.sum(expd, axis=1, keepdims=True))).astype(BF16)
        w_ref[at, :] = w
        mass_ref[...] += jnp.broadcast_to(jnp.sum(w.astype(F32), axis=0, keepdims=True), mass_ref.shape)
        for a in range(na):
            recon = nn(w, m_ref[a])
            res = (x_ref[a, at, :].astype(F32) - recon) * live
            r_ref[at, pl.ds(a * feats, feats)] = res.astype(BF16)

    core_peer, y_peer = q + 1 - 2 * lax.rem(q, 2), lax.rem(q + 2, na)
    x_bit = lax.rem(d, 2)
    x_peer = d + 1 - 2 * x_bit
    c_bit, y_bit, z = lax.rem(q, 2), q // 2, d // 2
    nz = n // 2

    def mass_copy(j, peer):
        return remote(mass_ref, masses.at[q], mass_send.at[j], mass_recv.at[q], (d, peer))

    masses[q] = mass_ref[...]
    for j in range(1, na):
        mass_copy(j, lax.rem(q + j, na)).start()

    for b in range(ents // 128):
        cols = slice(b * 128, (b + 1) * 128)
        wt_ref[cols, :] = w_ref[:, cols].T
    for t in range(2):
        a = (y_bit if t == 0 else 1 - y_bit) * 2 + 1 - c_bit
        s_send[t] = nn(wt_ref[...], x_ref[a])
    core_sums = remote(s_send, s_recv, st_send.at[0], st_recv.at[0], (d, core_peer))
    core_sums.start()

    out_rows = width // total
    for b in range(width // 128):
        cols = slice(b * 128, (b + 1) * 128)
        rt_ref[pl.ds(b * 128 // out_rows, 128 // out_rows)] = (
            r_ref[:, cols].T.reshape(128 // out_rows, out_rows, r_ref.shape[0])
        )

    def gram_rows(dx, dy, core):
        xb = x_bit if dx == 0 else 1 - x_bit
        yb = y_bit if dy == 0 else 1 - y_bit
        lhs = jnp.concatenate([rt_ref[(zz * 2 + xb) * na + yb * 2 + core] for zz in range(nz)], axis=0)
        return nn(lhs, r_ref[...])

    quarter = nz * out_rows
    order = ((1, 1), (1, 0), (0, 1), (0, 0))
    for i, (dx, dy) in enumerate(order):
        g_send[pl.ds(i * quarter, quarter), :] = gram_rows(dx, dy, 1 - c_bit).astype(BF16)
    core_gram = remote(g_send, g_recv, st_send.at[1], st_recv.at[1], (d, core_peer))
    core_gram.start()

    for t in range(2):
        a = (y_bit if t == 0 else 1 - y_bit) * 2 + c_bit
        s_keep[t] = nn(wt_ref[...], x_ref[a])
    core_sums.wait_recv()
    s_send2[...] = s_keep[1] + s_recv[1]
    y_sums = remote(s_send2, s_recv2, st_send.at[2], st_recv.at[2], (d, y_peer))
    y_sums.start()

    for i, (dx, dy) in enumerate(order):
        g_keep[pl.ds(i * quarter, quarter), :] = gram_rows(dx, dy, c_bit)
    core_gram.wait_recv()
    top = pl.ds(0, 2 * quarter)
    gx_send[...] = (g_keep[top, :] + g_recv[top, :].astype(F32)).astype(BF16)
    x_gram = remote(gx_send, gx_recv, st_send.at[3], st_recv.at[3], (x_peer, q))
    x_gram.start()
    low = pl.ds(2 * quarter, 2 * quarter)
    g_keep[low, :] += g_recv[low, :].astype(F32)
    x_gram.wait_recv()
    third, last = pl.ds(2 * quarter, quarter), pl.ds(3 * quarter, quarter)
    gy_send[...] = (g_keep[third, :] + gx_recv[pl.ds(0, quarter), :].astype(F32)).astype(BF16)
    y_gram = remote(gy_send, gy_recv, st_send.at[4], st_recv.at[4], (d, y_peer))
    y_gram.start()
    g_keep[last, :] += gx_recv[pl.ds(quarter, quarter), :].astype(F32)

    for j in range(1, na):
        src = lax.rem(q + j, na)
        remote(mass_ref, masses.at[src], mass_send.at[j], mass_recv.at[src], (d, src)).wait_recv()
    y_sums.wait_recv()
    mass = masses[0]
    for a in range(1, na):
        mass = mass + masses[a]
    col = jnp.broadcast_to(mass[:1, :], (128, ents)).T
    for b in range(feats // 128):
        cols = slice(b * 128, (b + 1) * 128)
        full = s_keep[0, :, cols] + s_recv[0, :, cols] + s_recv2[:, cols]
        new_ref[:, cols] = (full + 1.0 * means_ref[:, cols].astype(F32)) / (col + 1.0)

    y_gram.wait_recv()
    g_keep[last, :] += gy_recv[...].astype(F32)
    gz_send[...] = g_keep[last, :].astype(BF16)

    def z_copy(j):
        to = lax.rem(z + j, nz)
        return remote(
            gz_send.at[pl.ds(pl.multiple_of(to * out_rows, out_rows), out_rows), :],
            gz_recv.at[j - 1], gz_ssem.at[j - 1], gz_rsem.at[j - 1], (to * 2 + x_bit, q),
        )

    for j in range(1, nz):
        z_copy(j).start()
    acc = g_keep[pl.ds(pl.multiple_of(3 * quarter + z * out_rows, out_rows), out_rows), :]
    for j in range(1, nz):
        z_copy(j).wait_recv()
        acc = acc + gz_recv[j - 1].astype(F32)
    gram_ref[...] = acc / float(rec_dev * n)

    for j in range(1, na):
        mean_copy(j, lax.rem(q + j, na)).wait_send()
        mass_copy(j, lax.rem(q + j, na)).wait_send()
    for copy in (core_sums, core_gram, y_sums, x_gram, y_gram):
        copy.wait_send()
    for j in range(1, nz):
        z_copy(j).wait_send()

    @pl.loop(0, n)
    def _(k):
        o = lax.rem(d + half + k, n)

        @pl.when(k != half)
        def _():
            meta_copy(k).wait_send()

        for j in range(na):
            @pl.when(jnp.logical_not(jnp.logical_and(k == half, q == j)))
            def _():
                rec_copy(k, j, o).wait_send()


def fused(n, na, records, owner, entity_means, noise_bits):
    rec_dev, feats = records.shape
    ents = entity_means.shape[0]
    cap = 2 * rec_dev // n
    slots = 2 * rec_dev // na
    width = feats * na
    out_rows = width // (n * na)
    nz = n // 2
    quarter = nz * out_rows
    vm, dma = pltpu.VMEM, pltpu.SemaphoreType.DMA
    vspec = pl.BlockSpec(memory_space=pltpu.VMEM)
    scratch = [
        vm((1, rec_dev), jnp.int32), vm((n, 128), jnp.int32), vm((n, n, 128), jnp.int32),
        vm((n, cap, feats), BF16), vm((na, slots, feats), BF16), vm((na, ents, feats), BF16),
        vm((slots, ents), jnp.int32), vm((slots, ents), BF16), vm((ents, slots), BF16),
        vm((slots, width), BF16), vm((n * na, out_rows, slots), BF16),
        vm((8, ents), F32), vm((na, 8, ents), F32),
        vm((2, ents, feats), F32), vm((2, ents, feats), F32), vm((2, ents, feats), F32),
        vm((ents, feats), F32), vm((ents, feats), F32),
        vm((4 * quarter, width), BF16), vm((4 * quarter, width), F32), vm((4 * quarter, width), BF16),
        vm((2 * quarter, width), BF16), vm((2 * quarter, width), BF16),
        vm((quarter, width), BF16), vm((quarter, width), BF16),
        vm((quarter, width), BF16), vm((nz - 1, out_rows, width), BF16),
        dma((n, na)), dma((n, na)), dma((n,)), dma((n,)), dma((na,)), dma((na,)), dma((n,)),
        dma((na,)), dma((na,)), dma((5,)), dma((5,)), dma((nz - 1,)), dma((nz - 1,)),
    ]
    return pl.pallas_call(
        functools.partial(sweep_kernel, n, na),
        out_shape=(jax.ShapeDtypeStruct((ents, feats), F32), jax.ShapeDtypeStruct((out_rows, width), F32)),
        in_specs=[vspec, vspec, vspec, pl.BlockSpec(memory_space=pl.ANY)],
        out_specs=(vspec, vspec),
        scratch_shapes=scratch,
        compiler_params=pltpu.CompilerParams(
            collective_id=0, has_side_effects=True, vmem_limit_bytes=56 * 1024 * 1024
        ),
    )(owner.reshape(1, rec_dev), records, entity_means, noise_bits)


def sweep(records, owner, entity_means, noise_bits):
    n, na = lax.axis_size("dom"), lax.axis_size("attr")
    rec_dev, feats = records.shape
    sub = 2 * rec_dev // n // na
    out_rows = feats // n
    if na == 4 and n == 8 and sub % 16 == 0 and out_rows % 16 == 0:
        return fused(n, na, records, owner, entity_means, noise_bits)
    return shards(records, owner, entity_means, noise_bits)


def solution(mesh):
    in_specs = (P("dom", "attr"), P("dom", None), P("dom", "attr"), P("dom", None))
    out_specs = (P("dom", "attr"), P(("dom", "attr"), None))
    return jax.shard_map(sweep, mesh=mesh, in_specs=in_specs, out_specs=out_specs, check_vma=False)
```

```python
import functools

import jax
import jax.numpy as jnp
from jax import lax
from jax.experimental import pallas as pl
from jax.experimental.pallas import tpu as pltpu
from jax.sharding import PartitionSpec as P


def posterior(raw, bits, live, width):
    uniform = (bits.astype(jnp.float32) + 0.5) / 8192.0
    noise = -jnp.log(-jnp.log(uniform))
    logits = 3.0 * jnp.tanh(raw * width ** (-0.5)) + noise
    expd = jnp.exp(logits)
    return (expd / jnp.sum(expd, axis=1, keepdims=True) * live[:, None]).astype(jnp.bfloat16)


def shards(records, owner, entity_means, noise_bits):
    dom_count = lax.axis_size("dom")
    attr_count = lax.axis_size("attr")
    rec_dev, feat_cols = records.shape
    slot_count = 2 * rec_dev
    capacity = slot_count // dom_count
    width = feat_cols * attr_count
    total_records = rec_dev * dom_count
    dest = owner[:, 0]
    onehot = (dest[:, None] == jnp.arange(dom_count, dtype=jnp.int32)[None, :]).astype(jnp.int32)
    rank = jnp.sum(jnp.cumsum(onehot, axis=0) * onehot, axis=1) - 1
    position = dest * capacity + rank
    packed = jnp.zeros((slot_count, feat_cols), jnp.bfloat16).at[position].set(records)
    flag_buf = (
        jnp.zeros((slot_count,), jnp.bfloat16).at[position].set(jnp.ones((rec_dev,), jnp.bfloat16))
    )
    arrived, arrived_flags = (
        lax.all_to_all(
            packed.reshape(dom_count, capacity, feat_cols),
            "dom",
            split_axis=0,
            concat_axis=0,
            tiled=True,
        ),
        lax.all_to_all(
            flag_buf.reshape(dom_count, capacity), "dom", split_axis=0, concat_axis=0, tiled=True
        ),
    )
    arrived = arrived.reshape(slot_count, feat_cols)
    live = arrived_flags.reshape(slot_count).astype(jnp.float32)
    raw = lax.psum(jnp.dot(arrived, entity_means.T, preferred_element_type=jnp.float32), "attr")
    weights = posterior(raw, noise_bits, live, width)
    sums_cols = jnp.dot(weights.T, arrived, preferred_element_type=jnp.float32)
    mass_col = jnp.sum(weights.astype(jnp.float32), axis=0)[:, None]
    recon = jnp.dot(weights, entity_means, preferred_element_type=jnp.float32)
    col_resid = ((arrived.astype(jnp.float32) - recon) * live[:, None]).astype(jnp.bfloat16)
    residual = lax.all_to_all(col_resid, "attr", split_axis=0, concat_axis=1, tiled=True)
    new_means = (sums_cols + 1.0 * entity_means.astype(jnp.float32)) / (mass_col + 1.0)
    term = lax.dot_general(
        residual, residual, (((0,), (0,)), ((), ())), preferred_element_type=jnp.float32
    )
    gram = lax.psum_scatter(term / total_records, ("dom", "attr"), scatter_dimension=0, tiled=True)
    return (new_means, gram)

MESH = pl.DeviceIdType.MESH
F32, BF16 = jnp.float32, jnp.bfloat16
GROUP = 2
CHUNKS = 4


def nt(a, b):
    return lax.dot_general(a, b, (((1,), (1,)), ((), ())), preferred_element_type=F32)


def nn(a, b):
    return jnp.dot(a, b, preferred_element_type=F32)


def remote(src, dst, send_sem, recv_sem, dev):
    return pltpu.make_async_remote_copy(
        src_ref=src, dst_ref=dst, send_sem=send_sem, recv_sem=recv_sem, device_id=dev, device_id_type=MESH
    )


def sweep_kernel(
    n, na, owner_ref, records_ref, means_ref, noise_ref, new_ref, gram_ref,
    rank_ref, meta_ref, metas, packed, x_ref, m_ref, bits_ref, w_ref, wt_ref, r_ref, rt_ref,
    mass_ref, masses, s_send, s_keep, s_recv, s_send2, s_recv2,
    g_send, g_keep, g_recv, gx_send, gx_recv, gy_send, gy_recv, gz_send, gz_recv,
    rec_send, rec_recv, meta_send, meta_recv, mean_send, mean_recv, bits_sem,
    mass_send, mass_recv, sum_send, sum_recv, gc_ssem, gc_rsem, gx_ssem, gx_rsem, gy_ssem, gy_rsem,
    gz_ssem, gz_rsem,
):
    rec_dev, feats = records_ref.shape
    ents = means_ref.shape[0]
    cap = 2 * rec_dev // n
    sub = cap // na
    half = n // 2
    width = feats * na
    d, q = lax.axis_index("dom"), lax.axis_index("attr")
    me = d * na + q
    total = n * na

    barrier = pltpu.get_barrier_semaphore()

    @pl.loop(1, total)
    def _(i):
        dev = lax.rem(me + i, total)
        pl.semaphore_signal(barrier, inc=1, device_id=(dev // na, lax.rem(dev, na)), device_id_type=MESH)

    def bits_copy(k):
        s = lax.rem(d + half + n - k, n)
        rows = pl.ds(pl.multiple_of(s * cap + q * sub, sub), sub)
        return pltpu.make_async_copy(
            noise_ref.at[rows, :], bits_ref.at[pl.ds(pl.multiple_of(k * sub, sub), sub), :], bits_sem.at[k]
        )

    @pl.loop(0, n)
    def _(k):
        bits_copy(k).start()

    blk = 256
    ids = lax.broadcasted_iota(jnp.int32, (n, blk), 0)
    upper = (
        lax.broadcasted_iota(jnp.int32, (blk, blk), 0) <= lax.broadcasted_iota(jnp.int32, (blk, blk), 1)
    ).astype(F32).astype(BF16)
    carry = jnp.zeros((n, 1), F32)
    for b in range(rec_dev // blk):
        cols = slice(b * blk, (b + 1) * blk)
        hot = (ids == owner_ref[:, cols]).astype(F32)
        run = nn(hot.astype(BF16), upper) + carry
        rank_ref[:, cols] = (jnp.sum(run * hot, axis=0, keepdims=True) - 1.0).astype(jnp.int32)
        carry = carry + jnp.sum(hot, axis=1, keepdims=True)
    counts = jnp.broadcast_to(carry, (n, 128)).astype(jnp.int32)
    meta_ref[...] = counts
    metas[half] = counts
    m_ref[q] = means_ref[...]

    def mean_copy(j, peer):
        return remote(means_ref, m_ref.at[q], mean_send.at[j], mean_recv.at[q], (d, peer))

    def meta_copy(k):
        return remote(meta_ref, metas.at[k], meta_send.at[k], meta_recv.at[k], (lax.rem(d + half + k, n), q))

    def rec_copy(k, j, peer_d):
        return remote(
            packed.at[k, pl.ds(j * sub, sub), :],
            x_ref.at[q, pl.ds(pl.multiple_of(k * sub, sub), sub), :],
            rec_send.at[k, j], rec_recv.at[k, q], (peer_d, j),
        )

    def pack(k):
        o = lax.rem(d + half + k, n)
        pos = jnp.where(owner_ref[...] == o, rank_ref[...], -1)
        hot = (lax.broadcasted_iota(jnp.int32, (cap, rec_dev), 0) == pos).astype(F32).astype(BF16)
        packed[k] = nn(hot, records_ref[...]).astype(BF16)

    def dispatch(k):
        for j in range(na):
            mine = jnp.logical_and(k == half, q == j)

            @pl.when(jnp.logical_not(mine))
            def _():
                rec_copy(k, j, lax.rem(d + half + k, n)).start()

            @pl.when(mine)
            def _():
                x_ref[j, pl.ds(pl.multiple_of(k * sub, sub), sub), :] = packed[k, pl.ds(j * sub, sub), :]

        @pl.when(k != half)
        def _():
            meta_copy(k).start()

    pack(0)
    pl.semaphore_wait(barrier, total - 1)
    dispatch(0)
    for j in range(1, na):
        mean_copy(j, lax.rem(q + j, na)).start()

    @pl.loop(1, n)
    def _(k):
        pack(k)
        dispatch(k)

    for j in range(1, na):
        src = lax.rem(q + j, na)
        remote(means_ref, m_ref.at[src], mean_send.at[j], mean_recv.at[src], (d, src)).wait_recv()

    rows = GROUP * sub
    mass_ref[...] = jnp.zeros_like(mass_ref)

    @pl.loop(0, n // GROUP)
    def _(g):
        for t in range(GROUP):
            k = g * GROUP + t

            @pl.when(k != half)
            def _():
                meta_copy(k).wait_recv()

            bits_copy(k).wait()
            for a in range(na):
                @pl.when(jnp.logical_not(jnp.logical_and(k == half, q == a)))
                def _():
                    remote(
                        packed.at[k, pl.ds(0, sub), :],
                        x_ref.at[a, pl.ds(pl.multiple_of(k * sub, sub), sub), :],
                        rec_send.at[k, a], rec_recv.at[k, a], (d, a),
                    ).wait_recv()

        at = pl.ds(pl.multiple_of(g * rows, rows), rows)
        raw = nt(x_ref[0, at, :], m_ref[0])
        for a in range(1, na):
            raw = raw + nt(x_ref[a, at, :], m_ref[a])
        uniform = (bits_ref[at, :].astype(F32) + 0.5) / 8192.0
        expd = jnp.exp(3.0 * jnp.tanh(raw * width ** (-0.5))) / (-jnp.log(uniform))
        row = lax.broadcasted_iota(jnp.int32, (rows, 1), 0)
        live = jnp.zeros((rows, 1), F32)
        for t in range(GROUP):
            cnt = metas[g * GROUP + t, pl.ds(d, 1), :][:, :1]
            inside = jnp.logical_and(row >= t * sub, row < (t + 1) * sub)
            live = live + jnp.where(jnp.logical_and(inside, row - t * sub + q * sub < cnt), 1.0, 0.0)
        w = (expd * (live / jnp.sum(expd, axis=1, keepdims=True))).astype(BF16)
        w_ref[at, :] = w
        mass_ref[...] += jnp.broadcast_to(jnp.sum(w.astype(F32), axis=0, keepdims=True), mass_ref.shape)
        for a in range(na):
            recon = nn(w, m_ref[a])
            res = (x_ref[a, at, :].astype(F32) - recon) * live
            r_ref[at, pl.ds(a * feats, feats)] = res.astype(BF16)

    core_peer, y_peer = q + 1 - 2 * lax.rem(q, 2), lax.rem(q + 2, na)
    x_bit = lax.rem(d, 2)
    x_peer = d + 1 - 2 * x_bit
    c_bit, y_bit, z = lax.rem(q, 2), q // 2, d // 2
    nz = n // 2

    def mass_copy(j, peer):
        return remote(mass_ref, masses.at[q], mass_send.at[j], mass_recv.at[q], (d, peer))

    masses[q] = mass_ref[...]
    for j in range(1, na):
        mass_copy(j, lax.rem(q + j, na)).start()

    for b in range(ents // 128):
        cols = slice(b * 128, (b + 1) * 128)
        wt_ref[cols, :] = w_ref[:, cols].T

    def partial_sums(t, core):
        return nn(wt_ref[...], x_ref[(y_bit if t == 0 else 1 - y_bit) * 2 + core])

    def core_sums(t):
        return remote(s_send.at[t], s_recv.at[t], sum_send.at[t], sum_recv.at[t], (d, core_peer))

    for t in (1, 0):
        s_send[t] = partial_sums(t, 1 - c_bit)
        core_sums(t).start()
    s_keep[1] = partial_sums(1, c_bit)

    out_rows = width // total
    for b in range(width // 128):
        cols = slice(b * 128, (b + 1) * 128)
        rt_ref[pl.ds(b * 128 // out_rows, 128 // out_rows)] = (
            r_ref[:, cols].T.reshape(128 // out_rows, out_rows, r_ref.shape[0])
        )
    core_sums(1).wait_recv()
    s_send2[...] = s_keep[1] + s_recv[1]
    y_sums = remote(s_send2, s_recv2, sum_send.at[2], sum_recv.at[2], (d, y_peer))
    y_sums.start()

    quarter = nz * out_rows
    part = width // CHUNKS
    order = ((1, 1), (1, 0), (0, 1), (0, 0))

    def gram_rows(dx, dy, core, c):
        xb = x_bit if dx == 0 else 1 - x_bit
        yb = y_bit if dy == 0 else 1 - y_bit
        lhs = jnp.concatenate([rt_ref[(zz * 2 + xb) * na + yb * 2 + core] for zz in range(nz)], axis=0)
        return nn(lhs, r_ref[:, c * part:(c + 1) * part])

    def core_gram(c):
        return remote(g_send.at[c], g_recv.at[c], gc_ssem.at[c], gc_rsem.at[c], (d, core_peer))

    def x_gram(c):
        return remote(gx_send.at[c], gx_recv.at[c], gx_ssem.at[c], gx_rsem.at[c], (x_peer, q))

    def y_gram(c):
        return remote(gy_send.at[c], gy_recv.at[c], gy_ssem.at[c], gy_rsem.at[c], (d, y_peer))

    def z_copy(c, j):
        to = lax.rem(z + j, nz)
        return remote(
            gz_send.at[c, pl.ds(pl.multiple_of(to * out_rows, out_rows), out_rows), :],
            gz_recv.at[c, j - 1], gz_ssem.at[c, j - 1], gz_rsem.at[c, j - 1], (to * 2 + x_bit, q),
        )

    top, low = slice(0, 2 * quarter), slice(2 * quarter, 4 * quarter)
    third, last = slice(2 * quarter, 3 * quarter), slice(3 * quarter, 4 * quarter)

    def to_x(c):
        core_gram(c).wait_recv()
        gx_send[c] = (g_keep[c, top, :] + g_recv[c, top, :].astype(F32)).astype(BF16)
        x_gram(c).start()
        g_keep[c, low, :] += g_recv[c, low, :].astype(F32)

    def to_y(c):
        x_gram(c).wait_recv()
        gy_send[c] = (g_keep[c, third, :] + gx_recv[c, :quarter, :].astype(F32)).astype(BF16)
        y_gram(c).start()
        g_keep[c, last, :] += gx_recv[c, quarter:, :].astype(F32)

    def to_z(c):
        y_gram(c).wait_recv()
        gz_send[c] = g_keep[c, last, :] + gy_recv[c].astype(F32)
        for j in range(1, nz):
            z_copy(c, j).start()

    for c in range(CHUNKS):
        for i, (dx, dy) in enumerate(order):
            g_send[c, i * quarter:(i + 1) * quarter, :] = gram_rows(dx, dy, 1 - c_bit, c).astype(BF16)
        core_gram(c).start()
        for i, (dx, dy) in enumerate(order):
            g_keep[c, i * quarter:(i + 1) * quarter, :] = gram_rows(dx, dy, c_bit, c)
        if c > 0:
            to_x(c - 1)
    to_x(CHUNKS - 1)
    s_keep[0] = partial_sums(0, c_bit)
    core_sums(0).wait_recv()
    for c in range(CHUNKS):
        to_y(c)
        if c > 0:
            to_z(c - 1)

    for j in range(1, na):
        src = lax.rem(q + j, na)
        remote(mass_ref, masses.at[src], mass_send.at[j], mass_recv.at[src], (d, src)).wait_recv()
    y_sums.wait_recv()
    mass = masses[0]
    for a in range(1, na):
        mass = mass + masses[a]
    col = jnp.broadcast_to(mass[:1, :], (128, ents)).T
    for b in range(feats // 128):
        cols = slice(b * 128, (b + 1) * 128)
        full = s_keep[0, :, cols] + s_recv[0, :, cols] + s_recv2[:, cols]
        new_ref[:, cols] = (full + 1.0 * means_ref[:, cols].astype(F32)) / (col + 1.0)

    to_z(CHUNKS - 1)
    for c in range(CHUNKS):
        acc = gz_send[c, pl.ds(pl.multiple_of(z * out_rows, out_rows), out_rows), :]
        for j in range(1, nz):
            z_copy(c, j).wait_recv()
            acc = acc + gz_recv[c, j - 1]
        gram_ref[:, c * part:(c + 1) * part] = acc / float(rec_dev * n)

    for j in range(1, na):
        mean_copy(j, lax.rem(q + j, na)).wait_send()
        mass_copy(j, lax.rem(q + j, na)).wait_send()
    for copy in (core_sums(0), core_sums(1), y_sums):
        copy.wait_send()
    for c in range(CHUNKS):
        core_gram(c).wait_send()
        x_gram(c).wait_send()
        y_gram(c).wait_send()
        for j in range(1, nz):
            z_copy(c, j).wait_send()

    @pl.loop(0, n)
    def _(k):
        o = lax.rem(d + half + k, n)

        @pl.when(k != half)
        def _():
            meta_copy(k).wait_send()

        for j in range(na):
            @pl.when(jnp.logical_not(jnp.logical_and(k == half, q == j)))
            def _():
                rec_copy(k, j, o).wait_send()


def fused(n, na, records, owner, entity_means, noise_bits):
    rec_dev, feats = records.shape
    ents = entity_means.shape[0]
    cap = 2 * rec_dev // n
    slots = 2 * rec_dev // na
    width = feats * na
    out_rows = width // (n * na)
    nz = n // 2
    quarter = nz * out_rows
    part = width // CHUNKS
    vm, dma = pltpu.VMEM, pltpu.SemaphoreType.DMA
    vspec = pl.BlockSpec(memory_space=pltpu.VMEM)
    scratch = [
        vm((1, rec_dev), jnp.int32), vm((n, 128), jnp.int32), vm((n, n, 128), jnp.int32),
        vm((n, cap, feats), BF16), vm((na, slots, feats), BF16), vm((na, ents, feats), BF16),
        vm((slots, ents), jnp.int32), vm((slots, ents), BF16), vm((ents, slots), BF16),
        vm((slots, width), BF16), vm((n * na, out_rows, slots), BF16),
        vm((8, ents), F32), vm((na, 8, ents), F32),
        vm((2, ents, feats), F32), vm((2, ents, feats), F32), vm((2, ents, feats), F32),
        vm((ents, feats), F32), vm((ents, feats), F32),
        vm((CHUNKS, 4 * quarter, part), BF16), vm((CHUNKS, 4 * quarter, part), F32),
        vm((CHUNKS, 4 * quarter, part), BF16),
        vm((CHUNKS, 2 * quarter, part), BF16), vm((CHUNKS, 2 * quarter, part), BF16),
        vm((CHUNKS, quarter, part), BF16), vm((CHUNKS, quarter, part), BF16),
        vm((CHUNKS, quarter, part), F32), vm((CHUNKS, nz - 1, out_rows, part), F32),
        dma((n, na)), dma((n, na)), dma((n,)), dma((n,)), dma((na,)), dma((na,)), dma((n,)),
        dma((na,)), dma((na,)), dma((3,)), dma((3,)),
        *(dma((CHUNKS,)) for _ in range(6)), dma((CHUNKS, nz - 1)), dma((CHUNKS, nz - 1)),
    ]
    return pl.pallas_call(
        functools.partial(sweep_kernel, n, na),
        out_shape=(jax.ShapeDtypeStruct((ents, feats), F32), jax.ShapeDtypeStruct((out_rows, width), F32)),
        in_specs=[vspec, vspec, vspec, pl.BlockSpec(memory_space=pl.ANY)],
        out_specs=(vspec, vspec),
        scratch_shapes=scratch,
        compiler_params=pltpu.CompilerParams(
            collective_id=0, has_side_effects=True, vmem_limit_bytes=56 * 1024 * 1024
        ),
    )(owner.reshape(1, rec_dev), records, entity_means, noise_bits)


def sweep(records, owner, entity_means, noise_bits):
    n, na = lax.axis_size("dom"), lax.axis_size("attr")
    rec_dev, feats = records.shape
    sub = 2 * rec_dev // n // na
    out_rows = feats // n
    if na == 4 and n == 8 and sub % 16 == 0 and out_rows % 16 == 0:
        return fused(n, na, records, owner, entity_means, noise_bits)
    return shards(records, owner, entity_means, noise_bits)


def solution(mesh):
    in_specs = (P("dom", "attr"), P("dom", None), P("dom", "attr"), P("dom", None))
    out_specs = (P("dom", "attr"), P(("dom", "attr"), None))
    return jax.shard_map(sweep, mesh=mesh, in_specs=in_specs, out_specs=out_specs, check_vma=False)
```

```python
import functools

import jax
import jax.numpy as jnp
from jax import lax
from jax.experimental import pallas as pl
from jax.experimental.pallas import tpu as pltpu
from jax.sharding import PartitionSpec as P


def posterior(raw, bits, live, width):
    uniform = (bits.astype(jnp.float32) + 0.5) / 8192.0
    noise = -jnp.log(-jnp.log(uniform))
    logits = 3.0 * jnp.tanh(raw * width ** (-0.5)) + noise
    expd = jnp.exp(logits)
    return (expd / jnp.sum(expd, axis=1, keepdims=True) * live[:, None]).astype(jnp.bfloat16)


def shards(records, owner, entity_means, noise_bits):
    dom_count = lax.axis_size("dom")
    attr_count = lax.axis_size("attr")
    rec_dev, feat_cols = records.shape
    slot_count = 2 * rec_dev
    capacity = slot_count // dom_count
    width = feat_cols * attr_count
    total_records = rec_dev * dom_count
    dest = owner[:, 0]
    onehot = (dest[:, None] == jnp.arange(dom_count, dtype=jnp.int32)[None, :]).astype(jnp.int32)
    rank = jnp.sum(jnp.cumsum(onehot, axis=0) * onehot, axis=1) - 1
    position = dest * capacity + rank
    packed = jnp.zeros((slot_count, feat_cols), jnp.bfloat16).at[position].set(records)
    flag_buf = (
        jnp.zeros((slot_count,), jnp.bfloat16).at[position].set(jnp.ones((rec_dev,), jnp.bfloat16))
    )
    arrived, arrived_flags = (
        lax.all_to_all(
            packed.reshape(dom_count, capacity, feat_cols),
            "dom",
            split_axis=0,
            concat_axis=0,
            tiled=True,
        ),
        lax.all_to_all(
            flag_buf.reshape(dom_count, capacity), "dom", split_axis=0, concat_axis=0, tiled=True
        ),
    )
    arrived = arrived.reshape(slot_count, feat_cols)
    live = arrived_flags.reshape(slot_count).astype(jnp.float32)
    raw = lax.psum(jnp.dot(arrived, entity_means.T, preferred_element_type=jnp.float32), "attr")
    weights = posterior(raw, noise_bits, live, width)
    sums_cols = jnp.dot(weights.T, arrived, preferred_element_type=jnp.float32)
    mass_col = jnp.sum(weights.astype(jnp.float32), axis=0)[:, None]
    recon = jnp.dot(weights, entity_means, preferred_element_type=jnp.float32)
    col_resid = ((arrived.astype(jnp.float32) - recon) * live[:, None]).astype(jnp.bfloat16)
    residual = lax.all_to_all(col_resid, "attr", split_axis=0, concat_axis=1, tiled=True)
    new_means = (sums_cols + 1.0 * entity_means.astype(jnp.float32)) / (mass_col + 1.0)
    term = lax.dot_general(
        residual, residual, (((0,), (0,)), ((), ())), preferred_element_type=jnp.float32
    )
    gram = lax.psum_scatter(term / total_records, ("dom", "attr"), scatter_dimension=0, tiled=True)
    return (new_means, gram)

MESH = pl.DeviceIdType.MESH
F32, BF16 = jnp.float32, jnp.bfloat16
GROUP = 2
CHUNKS = 4


def nt(a, b):
    return lax.dot_general(a, b, (((1,), (1,)), ((), ())), preferred_element_type=F32)


def nn(a, b):
    return jnp.dot(a, b, preferred_element_type=F32)


def remote(src, dst, send_sem, recv_sem, dev):
    return pltpu.make_async_remote_copy(
        src_ref=src, dst_ref=dst, send_sem=send_sem, recv_sem=recv_sem, device_id=dev, device_id_type=MESH
    )


def sweep_kernel(
    n, na, owner_ref, records_ref, means_ref, noise_ref, new_ref, gram_ref,
    rank_ref, meta_ref, metas, packed, x_ref, m_ref, bits_ref, w_ref, wt_ref, r_ref, rt_ref,
    mass_ref, masses, s_send, s_keep, s_recv, s_send2, s_recv2,
    g_send, g_keep, g_recv, gx_send, gx_recv, gy_send, gy_recv, gz_send, gz_recv,
    rec_send, rec_recv, meta_send, meta_recv, mean_send, mean_recv, bits_sem,
    mass_send, mass_recv, sum_send, sum_recv, gc_ssem, gc_rsem, gx_ssem, gx_rsem, gy_ssem, gy_rsem,
    gz_ssem, gz_rsem, ys_ssem, ys_rsem,
):
    rec_dev, feats = records_ref.shape
    ents = means_ref.shape[0]
    cap = 2 * rec_dev // n
    sub = cap // na
    half = n // 2
    width = feats * na
    d, q = lax.axis_index("dom"), lax.axis_index("attr")
    me = d * na + q
    total = n * na

    barrier = pltpu.get_barrier_semaphore()

    @pl.loop(1, total)
    def _(i):
        dev = lax.rem(me + i, total)
        pl.semaphore_signal(barrier, inc=1, device_id=(dev // na, lax.rem(dev, na)), device_id_type=MESH)

    def bits_copy(k):
        s = lax.rem(d + half + n - k, n)
        rows = pl.ds(pl.multiple_of(s * cap + q * sub, sub), sub)
        return pltpu.make_async_copy(
            noise_ref.at[rows, :], bits_ref.at[pl.ds(pl.multiple_of(k * sub, sub), sub), :], bits_sem.at[k]
        )

    @pl.loop(0, n)
    def _(k):
        bits_copy(k).start()

    blk = 256
    ids = lax.broadcasted_iota(jnp.int32, (n, blk), 0)
    upper = (
        lax.broadcasted_iota(jnp.int32, (blk, blk), 0) <= lax.broadcasted_iota(jnp.int32, (blk, blk), 1)
    ).astype(F32).astype(BF16)
    carry = jnp.zeros((n, 1), F32)
    for b in range(rec_dev // blk):
        cols = slice(b * blk, (b + 1) * blk)
        hot = (ids == owner_ref[:, cols]).astype(F32)
        run = nn(hot.astype(BF16), upper) + carry
        rank_ref[:, cols] = (jnp.sum(run * hot, axis=0, keepdims=True) - 1.0).astype(jnp.int32)
        carry = carry + jnp.sum(hot, axis=1, keepdims=True)
    counts = jnp.broadcast_to(carry, (n, 128)).astype(jnp.int32)
    meta_ref[...] = counts
    metas[half] = counts
    m_ref[q] = means_ref[...]

    def mean_copy(j, peer):
        return remote(means_ref, m_ref.at[q], mean_send.at[j], mean_recv.at[q], (d, peer))

    def meta_copy(k):
        return remote(meta_ref, metas.at[k], meta_send.at[k], meta_recv.at[k], (lax.rem(d + half + k, n), q))

    def rec_copy(k, j, peer_d):
        return remote(
            packed.at[k, pl.ds(j * sub, sub), :],
            x_ref.at[q, pl.ds(pl.multiple_of(k * sub, sub), sub), :],
            rec_send.at[k, j], rec_recv.at[k, q], (peer_d, j),
        )

    def pack(k):
        o = lax.rem(d + half + k, n)
        pos = jnp.where(owner_ref[...] == o, rank_ref[...], -1)
        hot = (lax.broadcasted_iota(jnp.int32, (cap, rec_dev), 0) == pos).astype(F32).astype(BF16)
        packed[k] = nn(hot, records_ref[...]).astype(BF16)

    def dispatch(k):
        for j in range(na):
            mine = jnp.logical_and(k == half, q == j)

            @pl.when(jnp.logical_not(mine))
            def _():
                rec_copy(k, j, lax.rem(d + half + k, n)).start()

            @pl.when(mine)
            def _():
                x_ref[j, pl.ds(pl.multiple_of(k * sub, sub), sub), :] = packed[k, pl.ds(j * sub, sub), :]

        @pl.when(k != half)
        def _():
            meta_copy(k).start()

    pack(0)
    pl.semaphore_wait(barrier, total - 1)
    dispatch(0)
    for j in range(1, na):
        mean_copy(j, lax.rem(q + j, na)).start()

    @pl.loop(1, n)
    def _(k):
        pack(k)
        dispatch(k)

    for j in range(1, na):
        src = lax.rem(q + j, na)
        remote(means_ref, m_ref.at[src], mean_send.at[j], mean_recv.at[src], (d, src)).wait_recv()

    rows = GROUP * sub
    mass_ref[...] = jnp.zeros_like(mass_ref)

    @pl.loop(0, n // GROUP)
    def _(g):
        for t in range(GROUP):
            k = g * GROUP + t

            @pl.when(k != half)
            def _():
                meta_copy(k).wait_recv()

            bits_copy(k).wait()
            for a in range(na):
                @pl.when(jnp.logical_not(jnp.logical_and(k == half, q == a)))
                def _():
                    remote(
                        packed.at[k, pl.ds(0, sub), :],
                        x_ref.at[a, pl.ds(pl.multiple_of(k * sub, sub), sub), :],
                        rec_send.at[k, a], rec_recv.at[k, a], (d, a),
                    ).wait_recv()

        at = pl.ds(pl.multiple_of(g * rows, rows), rows)
        raw = nt(x_ref[0, at, :], m_ref[0])
        for a in range(1, na):
            raw = raw + nt(x_ref[a, at, :], m_ref[a])
        uniform = (bits_ref[at, :].astype(F32) + 0.5) / 8192.0
        expd = jnp.exp(3.0 * jnp.tanh(raw * width ** (-0.5))) / (-jnp.log(uniform))
        row = lax.broadcasted_iota(jnp.int32, (rows, 1), 0)
        live = jnp.zeros((rows, 1), F32)
        for t in range(GROUP):
            cnt = metas[g * GROUP + t, pl.ds(d, 1), :][:, :1]
            inside = jnp.logical_and(row >= t * sub, row < (t + 1) * sub)
            live = live + jnp.where(jnp.logical_and(inside, row - t * sub + q * sub < cnt), 1.0, 0.0)
        w = (expd * (live / jnp.sum(expd, axis=1, keepdims=True))).astype(BF16)
        w_ref[at, :] = w
        mass_ref[...] += jnp.broadcast_to(jnp.sum(w.astype(F32), axis=0, keepdims=True), mass_ref.shape)
        for a in range(na):
            recon = nn(w, m_ref[a])
            res = (x_ref[a, at, :].astype(F32) - recon) * live
            r_ref[at, pl.ds(a * feats, feats)] = res.astype(BF16)

    core_peer, y_peer = q + 1 - 2 * lax.rem(q, 2), lax.rem(q + 2, na)
    x_bit = lax.rem(d, 2)
    x_peer = d + 1 - 2 * x_bit
    c_bit, y_bit, z = lax.rem(q, 2), q // 2, d // 2
    nz = n // 2

    def mass_copy(j, peer):
        return remote(mass_ref, masses.at[q], mass_send.at[j], mass_recv.at[q], (d, peer))

    masses[q] = mass_ref[...]
    for j in range(1, na):
        mass_copy(j, lax.rem(q + j, na)).start()

    for b in range(ents // 128):
        cols = slice(b * 128, (b + 1) * 128)
        wt_ref[cols, :] = w_ref[:, cols].T

    def partial_sums(t, core):
        return nn(wt_ref[...], x_ref[(y_bit if t == 0 else 1 - y_bit) * 2 + core])

    def core_sums(t):
        return remote(s_send.at[t], s_recv.at[t], sum_send.at[t], sum_recv.at[t], (d, core_peer))

    for t in (1, 0):
        s_send[t] = partial_sums(t, 1 - c_bit)
        core_sums(t).start()
    s_keep[1] = partial_sums(1, c_bit)

    out_rows = width // total
    for b in range(width // 128):
        cols = slice(b * 128, (b + 1) * 128)
        rt_ref[pl.ds(b * 128 // out_rows, 128 // out_rows)] = (
            r_ref[:, cols].T.reshape(128 // out_rows, out_rows, r_ref.shape[0])
        )
    core_sums(1).wait_recv()
    s_send2[...] = s_keep[1] + s_recv[1]
    piece = ents // CHUNKS

    def y_sums(c):
        rows_c = pl.ds(c * piece, piece)
        return remote(s_send2.at[rows_c], s_recv2.at[rows_c], ys_ssem.at[c], ys_rsem.at[c], (d, y_peer))

    y_sums(0).start()

    quarter = nz * out_rows
    part = width // CHUNKS
    order = ((1, 1), (1, 0), (0, 1), (0, 0))

    def gram_rows(dx, dy, core, c):
        xb = x_bit if dx == 0 else 1 - x_bit
        yb = y_bit if dy == 0 else 1 - y_bit
        lhs = jnp.concatenate([rt_ref[(zz * 2 + xb) * na + yb * 2 + core] for zz in range(nz)], axis=0)
        return nn(lhs, r_ref[:, c * part:(c + 1) * part])

    def core_gram(c):
        return remote(g_send.at[c], g_recv.at[c], gc_ssem.at[c], gc_rsem.at[c], (d, core_peer))

    def x_gram(c):
        return remote(gx_send.at[c], gx_recv.at[c], gx_ssem.at[c], gx_rsem.at[c], (x_peer, q))

    def y_gram(c):
        return remote(gy_send.at[c], gy_recv.at[c], gy_ssem.at[c], gy_rsem.at[c], (d, y_peer))

    def z_copy(c, j):
        to = lax.rem(z + j, nz)
        return remote(
            gz_send.at[c, pl.ds(pl.multiple_of(to * out_rows, out_rows), out_rows), :],
            gz_recv.at[c, j - 1], gz_ssem.at[c, j - 1], gz_rsem.at[c, j - 1], (to * 2 + x_bit, q),
        )

    top, low = slice(0, 2 * quarter), slice(2 * quarter, 4 * quarter)
    third, last = slice(2 * quarter, 3 * quarter), slice(3 * quarter, 4 * quarter)

    def to_x(c):
        core_gram(c).wait_recv()
        gx_send[c] = (g_keep[c, top, :] + g_recv[c, top, :].astype(F32)).astype(BF16)
        x_gram(c).start()
        g_keep[c, low, :] += g_recv[c, low, :].astype(F32)

    def to_y(c):
        x_gram(c).wait_recv()
        gy_send[c] = (g_keep[c, third, :] + gx_recv[c, :quarter, :].astype(F32)).astype(BF16)
        y_gram(c).start()
        if c + 1 < CHUNKS:
            y_sums(c + 1).start()
        g_keep[c, last, :] += gx_recv[c, quarter:, :].astype(F32)

    def to_z(c):
        y_gram(c).wait_recv()
        gz_send[c] = g_keep[c, last, :] + gy_recv[c].astype(F32)
        for j in range(1, nz):
            z_copy(c, j).start()

    for c in range(CHUNKS):
        for i, (dx, dy) in enumerate(order):
            g_send[c, i * quarter:(i + 1) * quarter, :] = gram_rows(dx, dy, 1 - c_bit, c).astype(BF16)
        core_gram(c).start()
        for i, (dx, dy) in enumerate(order):
            g_keep[c, i * quarter:(i + 1) * quarter, :] = gram_rows(dx, dy, c_bit, c)
        if c > 0:
            to_x(c - 1)
    to_x(CHUNKS - 1)
    s_keep[0] = partial_sums(0, c_bit)
    core_sums(0).wait_recv()
    for c in range(CHUNKS):
        to_y(c)
        if c > 0:
            to_z(c - 1)

    for j in range(1, na):
        src = lax.rem(q + j, na)
        remote(mass_ref, masses.at[src], mass_send.at[j], mass_recv.at[src], (d, src)).wait_recv()
    for c in range(CHUNKS):
        y_sums(c).wait_recv()
    mass = masses[0]
    for a in range(1, na):
        mass = mass + masses[a]
    col = jnp.broadcast_to(mass[:1, :], (128, ents)).T
    for b in range(feats // 128):
        cols = slice(b * 128, (b + 1) * 128)
        full = s_keep[0, :, cols] + s_recv[0, :, cols] + s_recv2[:, cols]
        new_ref[:, cols] = (full + 1.0 * means_ref[:, cols].astype(F32)) / (col + 1.0)

    to_z(CHUNKS - 1)
    for c in range(CHUNKS):
        acc = gz_send[c, pl.ds(pl.multiple_of(z * out_rows, out_rows), out_rows), :]
        for j in range(1, nz):
            z_copy(c, j).wait_recv()
            acc = acc + gz_recv[c, j - 1]
        gram_ref[:, c * part:(c + 1) * part] = acc

    for j in range(1, na):
        mean_copy(j, lax.rem(q + j, na)).wait_send()
        mass_copy(j, lax.rem(q + j, na)).wait_send()
    for t in range(2):
        core_sums(t).wait_send()
    for c in range(CHUNKS):
        y_sums(c).wait_send()
        core_gram(c).wait_send()
        x_gram(c).wait_send()
        y_gram(c).wait_send()
        for j in range(1, nz):
            z_copy(c, j).wait_send()

    @pl.loop(0, n)
    def _(k):
        o = lax.rem(d + half + k, n)

        @pl.when(k != half)
        def _():
            meta_copy(k).wait_send()

        for j in range(na):
            @pl.when(jnp.logical_not(jnp.logical_and(k == half, q == j)))
            def _():
                rec_copy(k, j, o).wait_send()


def finish_kernel(records, means_ref, gram_ref, means_out, gram_out):
    means_out[...] = means_ref[...]
    gram_out[...] = gram_ref[...] / records


def fused(n, na, records, owner, entity_means, noise_bits):
    rec_dev, feats = records.shape
    ents = entity_means.shape[0]
    cap = 2 * rec_dev // n
    slots = 2 * rec_dev // na
    width = feats * na
    out_rows = width // (n * na)
    nz = n // 2
    quarter = nz * out_rows
    part = width // CHUNKS
    vm, dma = pltpu.VMEM, pltpu.SemaphoreType.DMA
    vspec = pl.BlockSpec(memory_space=pltpu.VMEM)
    scratch = [
        vm((1, rec_dev), jnp.int32), vm((n, 128), jnp.int32), vm((n, n, 128), jnp.int32),
        vm((n, cap, feats), BF16), vm((na, slots, feats), BF16), vm((na, ents, feats), BF16),
        vm((slots, ents), jnp.int32), vm((slots, ents), BF16), vm((ents, slots), BF16),
        vm((slots, width), BF16), vm((n * na, out_rows, slots), BF16),
        vm((8, ents), F32), vm((na, 8, ents), F32),
        vm((2, ents, feats), F32), vm((2, ents, feats), F32), vm((2, ents, feats), F32),
        vm((ents, feats), F32), vm((ents, feats), F32),
        vm((CHUNKS, 4 * quarter, part), BF16), vm((CHUNKS, 4 * quarter, part), F32),
        vm((CHUNKS, 4 * quarter, part), BF16),
        vm((CHUNKS, 2 * quarter, part), BF16), vm((CHUNKS, 2 * quarter, part), BF16),
        vm((CHUNKS, quarter, part), BF16), vm((CHUNKS, quarter, part), BF16),
        vm((CHUNKS, quarter, part), F32), vm((CHUNKS, nz - 1, out_rows, part), F32),
        dma((n, na)), dma((n, na)), dma((n,)), dma((n,)), dma((na,)), dma((na,)), dma((n,)),
        dma((na,)), dma((na,)), dma((2,)), dma((2,)),
        *(dma((CHUNKS,)) for _ in range(6)), dma((CHUNKS, nz - 1)), dma((CHUNKS, nz - 1)),
        dma((CHUNKS,)), dma((CHUNKS,)),
    ]
    new_means, gram = pl.pallas_call(
        functools.partial(sweep_kernel, n, na),
        out_shape=(jax.ShapeDtypeStruct((ents, feats), F32), jax.ShapeDtypeStruct((out_rows, width), F32)),
        in_specs=[vspec, vspec, vspec, pl.BlockSpec(memory_space=pl.ANY)],
        out_specs=(vspec, vspec),
        scratch_shapes=scratch,
        compiler_params=pltpu.CompilerParams(
            collective_id=0, has_side_effects=True, vmem_limit_bytes=56 * 1024 * 1024
        ),
    )(owner.reshape(1, rec_dev), records, entity_means, noise_bits)
    return pl.pallas_call(
        functools.partial(finish_kernel, float(rec_dev * n)),
        out_shape=(jax.ShapeDtypeStruct((ents, feats), F32), jax.ShapeDtypeStruct((out_rows, width), F32)),
        in_specs=[vspec, vspec],
        out_specs=(vspec, vspec),
    )(new_means, gram)


def sweep(records, owner, entity_means, noise_bits):
    n, na = lax.axis_size("dom"), lax.axis_size("attr")
    rec_dev, feats = records.shape
    sub = 2 * rec_dev // n // na
    out_rows = feats // n
    if na == 4 and n == 8 and sub % 16 == 0 and out_rows % 16 == 0:
        return fused(n, na, records, owner, entity_means, noise_bits)
    return shards(records, owner, entity_means, noise_bits)


def solution(mesh):
    in_specs = (P("dom", "attr"), P("dom", None), P("dom", "attr"), P("dom", None))
    out_specs = (P("dom", "attr"), P(("dom", "attr"), None))
    return jax.shard_map(sweep, mesh=mesh, in_specs=in_specs, out_specs=out_specs, check_vma=False)
```
